32 devices in a mesh: dp: 8 (over y, x, core), tensor: 4 (over z).
Axes of the slice: x: 2, y: 2, z: 4, core: 2. Of those that a mesh axis runs over, the one named last changes fastest.
Arguments:
- teacher_hidden: bfloat16 [1024, 4096], P('dp'), may hold values from -6 to 6
- student_hidden: bfloat16 [1024, 2048], P('dp'), may hold values from -6 to 6
- target_ids: int32 [1024], P('dp'), may hold values from 0 to 64127
- teacher_head: bfloat16 [4096, 65536], P(None, ('dp', 'tensor')), may hold values from -1 to 1
- student_head: bfloat16 [2048, 65536], P(None, ('dp', 'tensor')), may hold values from -1 to 1
Outputs:
- head_grad: float32 [2048, 65536], P(None, ('dp', 'tensor'))
- input_grad: float32 [1024, 2048], P('dp', 'tensor')
The draws below stay inside these ranges and needn't reach their ends.
All inputs are finite; a program needn't handle non-finite values.
Results may differ from the reference program's by a relative error of at most 0.0065.
Values may be sent and summed in bfloat16 or wider, within the bound.
A program may use at most 128 MiB of HBM per device.

```python
import math
import jax
import jax.numpy as jnp
import numpy as np
from jax import lax

DT = 4096
DS = 2048
VOCAB = 64128
PADDED = 65536
TOKENS = 1024


def column_vectors(head_key, depth, indices):
    scale = 4.0 / jnp.sqrt(jnp.float32(depth))
    one_column = lambda index: jax.random.normal(jax.random.fold_in(head_key, index), (depth,), jnp.float32)
    return jax.vmap(one_column)(indices) * scale


def head_matrix(key, salt, depth):
    head_key = jax.random.fold_in(key, salt)
    columns = column_vectors(head_key, depth, jnp.arange(PADDED, dtype=jnp.int32))
    return jnp.clip(columns.T, -1.0, 1.0).astype(jnp.bfloat16)


def hidden_rows(key, salt, depth):
    drawn_rows = jnp.clip(jax.random.normal(jax.random.fold_in(key, salt), (TOKENS, depth), jnp.float32), -6.0, 6.0)
    return drawn_rows.astype(jnp.bfloat16)


def draw_teacher_head(key, part):
    return head_matrix(key, 101, DT)


def draw_student_head(key, part):
    return head_matrix(key, 202, DS)


def draw_teacher_hidden(key, part):
    return hidden_rows(key, 303, DT)


def draw_student_hidden(key, part):
    return hidden_rows(key, 404, DS)


def plant(drawn, own_key, least, top_value):
    longest = drawn.shape.index(max(drawn.shape))
    spots = []
    for shift in (0, 1):
        where = [jax.random.randint(jax.random.fold_in(own_key, axis), (), 0, length) for axis, length in enumerate(drawn.shape)]
        where[longest] = (where[longest] + shift) % drawn.shape[longest]
        spots.append(tuple(where))
    return drawn.at[spots[0]].set(least).at[spots[1]].set(top_value)


def rank_table(number_of, slope):
    portions = [(1 << 20) // math.isqrt(standing ** slope) + 1 for standing in range(1, number_of + 1)]
    scale = 1 + sum(portions) // (1 << 30)
    return np.cumsum(np.array([max(1, weight // scale) for weight in portions]))


def ranked_ids(stream_key, extent, count, slope):
    table = rank_table(count, slope)
    pick = jax.random.randint(jax.random.fold_in(stream_key, 1), extent, 0, int(table[count - 1]))
    rank = jnp.searchsorted(jnp.asarray(table, jnp.int32), pick, side="right")
    return jax.random.permutation(jax.random.fold_in(stream_key, 2), count)[rank].astype(jnp.int32)


def setup_inputs(seed: int = 0) -> dict:
    streams_of = jax.random.split(jax.random.key(seed), 6)
    teacher_hidden = draw_teacher_hidden(jax.random.fold_in(streams_of[5], 71), 0)
    student_hidden = draw_student_hidden(jax.random.fold_in(streams_of[5], 71), 0)
    target_ids = plant(ranked_ids(streams_of[2], (TOKENS,), VOCAB, 2), jax.random.fold_in(streams_of[2], 3), 0, VOCAB - 1).astype(jnp.int32)
    teacher_head = draw_teacher_head(jax.random.fold_in(streams_of[5], 71), 0)
    student_head = draw_student_head(jax.random.fold_in(streams_of[5], 71), 0)
    return {"teacher_hidden": teacher_hidden, "student_hidden": student_hidden, "target_ids": target_ids, "teacher_head": teacher_head, "student_head": student_head}


def softmax_rows(logits):
    peak = jnp.max(logits, axis=1, keepdims=True)
    expo = jnp.exp(logits - peak)
    return expo / jnp.sum(expo, axis=1, keepdims=True)


def reference(teacher_hidden, student_hidden, target_ids, teacher_head, student_head):
    columns = jnp.arange(PADDED, dtype=jnp.int32)
    is_real = (columns < VOCAB)[None, :]
    teacher_logits = jnp.where(is_real, jnp.dot(teacher_hidden, teacher_head, preferred_element_type=jnp.float32), jnp.float32(-1e30))
    student_logits = jnp.where(is_real, jnp.dot(student_hidden, student_head, preferred_element_type=jnp.float32), jnp.float32(-1e30))
    teacher_probs = softmax_rows(teacher_logits)
    student_probs = softmax_rows(student_logits)
    onehot = (target_ids[:, None] == columns[None, :]).astype(jnp.float32)
    logit_grad = (2.0 * student_probs - teacher_probs - onehot).astype(jnp.bfloat16)
    head_grad = lax.dot_general(student_hidden, logit_grad, (((0,), (0,)), ((), ())), preferred_element_type=jnp.float32)
    input_grad = lax.dot_general(logit_grad, student_head, (((1,), (1,)), ((), ())), preferred_element_type=jnp.float32)
    return head_grad, input_grad
```

```python
import jax
import jax.numpy as jnp
from jax import lax
from jax.sharding import PartitionSpec as P

VOCAB = 64128


def body(teacher_hidden, student_hidden, target_ids, teacher_head, student_head):
    width_cols = teacher_head.shape[1]
    first_col = (
        lax.axis_index("dp") * lax.axis_size("tensor") + lax.axis_index("tensor")
    ) * width_cols
    columns = first_col + lax.iota(jnp.int32, width_cols)
    is_real = (columns < VOCAB)[None, :]
    teacher_logits = jnp.dot(
        lax.all_gather(teacher_hidden, "dp", axis=0, tiled=True),
        teacher_head,
        preferred_element_type=jnp.float32,
    )
    teacher_logits = jnp.where(is_real, teacher_logits, jnp.float32(-1e30))
    student_rows, all_targets = (
        lax.all_gather(student_hidden, "dp", axis=0, tiled=True),
        lax.all_gather(target_ids, "dp", axis=0, tiled=True),
    )
    student_logits = jnp.where(
        is_real,
        jnp.dot(student_rows, student_head, preferred_element_type=jnp.float32),
        jnp.float32(-1e30),
    )
    peaks = jnp.stack([jnp.max(teacher_logits, axis=1), jnp.max(student_logits, axis=1)])
    totals = jnp.stack(
        [
            jnp.sum(jnp.exp(teacher_logits - peaks[0][:, None]), axis=1),
            jnp.sum(jnp.exp(student_logits - peaks[1][:, None]), axis=1),
        ]
    )
    table = lax.all_gather(jnp.concatenate([peaks, totals]), ("dp", "tensor"), axis=0)
    top = jnp.max(table[:, :2], axis=0)
    teacher_total, student_total = jnp.sum(table[:, 2:] * jnp.exp(table[:, :2] - top), axis=0)
    teacher_expo = jnp.exp(teacher_logits - top[0][:, None])
    student_expo = jnp.exp(student_logits - top[1][:, None])
    teacher_probs = teacher_expo / teacher_total[:, None]
    student_probs = student_expo / student_total[:, None]
    onehot = (all_targets[:, None] == columns[None, :]).astype(jnp.float32)
    logit_grad = (2.0 * student_probs - teacher_probs - onehot).astype(jnp.bfloat16)
    head_grad = lax.dot_general(
        student_rows, logit_grad, (((0,), (0,)), ((), ())), preferred_element_type=jnp.float32
    )
    own_rows = lax.psum_scatter(
        lax.dot_general(
            logit_grad, student_head, (((1,), (1,)), ((), ())), preferred_element_type=jnp.float32
        ),
        "dp",
        scatter_dimension=0,
        tiled=True,
    )
    input_grad = lax.psum_scatter(own_rows, "tensor", scatter_dimension=1, tiled=True)
    return (head_grad, input_grad)


def solution(mesh):
    placed = (
        P("dp", None),
        P("dp", None),
        P("dp"),
        P(None, ("dp", "tensor")),
        P(None, ("dp", "tensor")),
    )
    return jax.shard_map(
        body,
        mesh=mesh,
        in_specs=placed,
        out_specs=(P(None, ("dp", "tensor")), P("dp", "tensor")),
        check_vma=False,
    )
```

```python
import functools

import jax
import jax.numpy as jnp
from jax import lax
from jax.experimental import pallas as pl
from jax.experimental.pallas import tpu as pltpu
from jax.sharding import PartitionSpec as P

VOCAB = 64128


def body(teacher_hidden, student_hidden, target_ids, teacher_head, student_head):
    width_cols = teacher_head.shape[1]
    first_col = (
        lax.axis_index("dp") * lax.axis_size("tensor") + lax.axis_index("tensor")
    ) * width_cols
    columns = first_col + lax.iota(jnp.int32, width_cols)
    is_real = (columns < VOCAB)[None, :]
    teacher_logits = jnp.dot(
        lax.all_gather(teacher_hidden, "dp", axis=0, tiled=True),
        teacher_head,
        preferred_element_type=jnp.float32,
    )
    teacher_logits = jnp.where(is_real, teacher_logits, jnp.float32(-1e30))
    student_rows, all_targets = (
        lax.all_gather(student_hidden, "dp", axis=0, tiled=True),
        lax.all_gather(target_ids, "dp", axis=0, tiled=True),
    )
    student_logits = jnp.where(
        is_real,
        jnp.dot(student_rows, student_head, preferred_element_type=jnp.float32),
        jnp.float32(-1e30),
    )
    peaks = jnp.stack([jnp.max(teacher_logits, axis=1), jnp.max(student_logits, axis=1)])
    totals = jnp.stack(
        [
            jnp.sum(jnp.exp(teacher_logits - peaks[0][:, None]), axis=1),
            jnp.sum(jnp.exp(student_logits - peaks[1][:, None]), axis=1),
        ]
    )
    table = lax.all_gather(jnp.concatenate([peaks, totals]), ("dp", "tensor"), axis=0)
    top = jnp.max(table[:, :2], axis=0)
    teacher_total, student_total = jnp.sum(table[:, 2:] * jnp.exp(table[:, :2] - top), axis=0)
    teacher_expo = jnp.exp(teacher_logits - top[0][:, None])
    student_expo = jnp.exp(student_logits - top[1][:, None])
    teacher_probs = teacher_expo / teacher_total[:, None]
    student_probs = student_expo / student_total[:, None]
    onehot = (all_targets[:, None] == columns[None, :]).astype(jnp.float32)
    logit_grad = (2.0 * student_probs - teacher_probs - onehot).astype(jnp.bfloat16)
    head_grad = lax.dot_general(
        student_rows, logit_grad, (((0,), (0,)), ((), ())), preferred_element_type=jnp.float32
    )
    own_rows = lax.psum_scatter(
        lax.dot_general(
            logit_grad, student_head, (((1,), (1,)), ((), ())), preferred_element_type=jnp.float32
        ),
        "dp",
        scatter_dimension=0,
        tiled=True,
    )
    input_grad = lax.psum_scatter(own_rows, "tensor", scatter_dimension=1, tiled=True)
    return (head_grad, input_grad)


MESH = pl.DeviceIdType.MESH
LINKED = 9


def as_column(row):
    return jnp.transpose(jnp.broadcast_to(row, (row.shape[1], row.shape[1])))[:, :1]


def as_row(column):
    return jnp.transpose(jnp.broadcast_to(column, (column.shape[0], column.shape[0])))[:1, :]


def kernel(
    n, nt, tile,
    teacher_in, student_in, ids_in, teacher_head, student_head,
    grad_out, rows_out, input_out,
    t_rows, s_rows, ids, t_w, s_w, t_exp, s_exp,
    stats, local_peak, stats_in, scale, pair_in, plane_in, line_in,
    local_sem, out_sem, gather_send, gather_recv, ids_send, ids_recv,
    stats_send, stats_recv, pair_send, pair_recv, plane_send, plane_recv, line_send, line_recv,
):
    block = teacher_in.shape[0]
    pair = 2 * block
    width = t_w.shape[1]
    depth = s_w.shape[0]
    features = depth // nt
    dp = lax.axis_index("dp")
    tz = lax.axis_index("tensor")
    chip, core = dp // 2, dp % 2

    def flip(value, bit):
        return value + bit - 2 * bit * ((value // bit) % 2)

    def other(d):
        out = chip
        for bit in (1, 2):
            if d & bit:
                out = flip(out, bit)
        return out

    sibling = chip * 2 + 1 - core
    near = (other(1) * 2 + core, other(2) * 2 + core)

    barrier = pltpu.get_barrier_semaphore()
    for k in range(1, n):
        pl.semaphore_signal(barrier, inc=1, device_id=(lax.rem(dp + k, n), tz), device_id_type=MESH)
    for k in range(1, nt):
        pl.semaphore_signal(barrier, inc=1, device_id=(dp, lax.rem(tz + k, nt)), device_id_type=MESH)
    pl.semaphore_wait(barrier, n - 1 + nt - 1)

    def at(index, start=0, size=None):
        return pl.ds(pl.multiple_of(index * block + start, block // 2), block if size is None else size)

    def remote(source, target, send, recv, device):
        return pltpu.make_async_remote_copy(
            src_ref=source, dst_ref=target, send_sem=send, recv_sem=recv,
            device_id=device, device_id_type=MESH,
        )

    def message(k, rows, device, from_input=False):
        pieces = []
        for a, (given, held) in enumerate(((student_in, s_rows), (teacher_in, t_rows))):
            source = given if from_input else held.at[rows]
            pieces.append(
                remote(source, held.at[rows], gather_send.at[k, a], gather_recv.at[k, a], (device, tz))
            )
        return pieces

    own = at(dp)
    msgs = [message(0, own, sibling, True), message(1, own, near[0], True), message(2, own, near[1], True)]
    for a in range(2):
        for m in (msgs[1], msgs[2], msgs[0]):
            m[a].start()
    loads = [
        pltpu.make_async_copy(student_in, s_rows.at[own], local_sem.at[0]),
        pltpu.make_async_copy(student_head, s_w, local_sem.at[1]),
        pltpu.make_async_copy(teacher_in, t_rows.at[own], local_sem.at[2]),
        pltpu.make_async_copy(teacher_head, t_w, local_sem.at[3]),
        pltpu.make_async_copy(ids_in, ids.at[dp], local_sem.at[4]),
    ]
    for load in loads:
        load.start()
    id_msgs = []
    for k in range(1, n):
        id_msgs.append(
            remote(ids_in, ids.at[dp], ids_send.at[k - 1], ids_recv.at[k - 1], (lax.rem(dp + k, n), tz))
        )
        id_msgs[-1].start()

    first_col = (dp * nt + tz) * width

    def forward(which, d):
        rows_ref, w_ref, exp_ref = ((s_rows, s_w, s_exp), (t_rows, t_w, t_exp))[which]
        target = other(d)
        rows = pl.ds(pl.multiple_of(target * pair, pair), pair)

        def multiply(j, peak):
            cols = pl.ds(pl.multiple_of(j * tile, tile), tile)
            z = jnp.dot(rows_ref[rows, :], w_ref[:, cols], preferred_element_type=jnp.float32)
            col = first_col + j * tile + lax.broadcasted_iota(jnp.int32, (1, tile), 1)
            z = jnp.where(col < VOCAB, z, jnp.float32(-1e30))
            exp_ref[rows, cols] = z
            return jnp.maximum(peak, jnp.max(z, axis=1, keepdims=True))

        peak = lax.fori_loop(0, width // tile, multiply, jnp.full((pair, 1), -jnp.inf, jnp.float32))

        def exponential(j, total):
            cols = pl.ds(pl.multiple_of(j * tile, tile), tile)
            e = jnp.exp(exp_ref[rows, cols] - peak)
            exp_ref[rows, cols] = e
            return total + jnp.sum(e, axis=1, keepdims=True)

        total = lax.fori_loop(0, width // tile, exponential, jnp.zeros((pair, 1), jnp.float32))
        for h in range(2):
            slot = pl.ds((1 - which) * n + target * 2 + h, 1)
            stats[0, slot, :] = as_row(peak[h * block : (h + 1) * block])
            stats[1, slot, :] = as_row(total[h * block : (h + 1) * block])

    loads[0].wait()
    loads[1].wait()
    msgs[0][0].wait_recv()
    forward(0, 0)
    loads[2].wait()
    loads[3].wait()
    msgs[0][1].wait_recv()
    forward(1, 0)

    half = block // 2
    across = other(3) * 2 + core
    msgs.append(message(3, at(near[0], 0, half), near[1]))
    msgs.append(message(4, at(near[1], half, half), near[0]))
    msgs.append(message(5, at(near[0]), sibling))
    msgs.append(message(6, at(near[1]), sibling))
    msgs.append(message(7, at(across, 0, half), sibling))
    msgs.append(message(8, at(across, half, half), sibling))
    for a in range(2):
        for k in (1, 2):
            msgs[k][a].wait_recv()
            msgs[k + 2][a].start()
            msgs[k + 4][a].start()
    for a in range(2):
        msgs[5][a].wait_recv()
        forward(a, 1)
    msgs[6][0].wait_recv()
    forward(0, 2)
    for k in (3, 4):
        msgs[k][0].wait_recv()
        msgs[k + 4][0].start()
    msgs[6][1].wait_recv()
    forward(1, 2)
    for k in (3, 4):
        msgs[k][1].wait_recv()
        msgs[k + 4][1].start()
    for a in range(2):
        msgs[7][a].wait_recv()
        msgs[8][a].wait_recv()
        forward(a, 3)
    rows_copy = pltpu.make_async_copy(s_rows, rows_out, out_sem.at[4])
    rows_copy.start()

    local_peak[...] = stats[0]
    partners = []
    bit = 1
    while bit < n:
        partners.append((flip(dp, bit), tz))
        bit *= 2
    bit = 1
    while bit < nt:
        partners.append((dp, flip(tz, bit)))
        bit *= 2
    for r, partner in enumerate(partners):
        swap = remote(stats, stats_in.at[r], stats_send.at[r], stats_recv.at[r], partner)
        swap.start()
        swap.wait()
        mine, theirs = stats[0], stats_in[r, 0]
        top = jnp.maximum(mine, theirs)
        stats[1] = stats[1] * jnp.exp(mine - top) + stats_in[r, 1] * jnp.exp(theirs - top)
        stats[0] = top
    scale[...] = jnp.exp(local_peak[...] - stats[0]) / stats[1]
    loads[4].wait()
    for m in id_msgs:
        m.wait()
    for m in msgs:
        for piece in m:
            piece.wait_send()

    tokens = t_rows.shape[0]
    grads = t_w
    outs, pairs, planes = [], {}, {}

    def plane_rows(d):
        return pl.ds(tokens + (d - 1) * block, block)

    def reduce_pair(d):
        pairs[d].wait()
        mine = pl.ds(pl.multiple_of(other(d) * pair + core * block, block), block)
        if d:
            grads[plane_rows(d), :] = (t_exp[mine, :] + pair_in[d]).astype(jnp.bfloat16)
            planes[d] = remote(
                grads.at[plane_rows(d)], plane_in.at[d - 1],
                plane_send.at[d - 1], plane_recv.at[d - 1], (other(d) * 2 + core, tz),
            )
            planes[d].start()

    waiting = None
    for d in (3, 1, 2, 0):
        target = other(d)
        rows = pl.ds(pl.multiple_of(target * pair, pair), pair)

        def column_of(ref_row):
            return jnp.concatenate([as_column(ref_row(h)) for h in range(2)], axis=0)

        t_scale = column_of(lambda h: scale[pl.ds(target * 2 + h, 1), :])
        s_scale = 2.0 * column_of(lambda h: scale[pl.ds(n + target * 2 + h, 1), :])
        wanted = column_of(lambda h: ids[target * 2 + h][:1, :])

        def gradient(j, carry):
            cols = pl.ds(pl.multiple_of(j * tile, tile), tile)
            col = (first_col + j * tile + lax.broadcasted_iota(jnp.int32, (1, tile), 1)).astype(jnp.float32)
            g = s_exp[rows, cols] * s_scale - t_exp[rows, cols] * t_scale
            g = g - jnp.where(wanted == col, 1.0, 0.0)
            grads[rows, cols] = g.astype(jnp.bfloat16)
            return carry

        lax.fori_loop(0, width // tile, gradient, 0)
        outs.append(pltpu.make_async_copy(grads.at[rows], grad_out.at[rows], out_sem.at[d]))
        outs[-1].start()

        def back(j, carry):
            cols = pl.ds(pl.multiple_of(j * tile, tile), tile)
            t_exp[rows, cols] = lax.dot_general(
                grads[rows, :], s_w[cols, :], (((1,), (1,)), ((), ())), preferred_element_type=jnp.float32
            )
            return carry

        lax.fori_loop(0, depth // tile, back, 0)
        theirs = pl.ds(pl.multiple_of(target * pair + (1 - core) * block, block), block)
        pairs[d] = remote(t_exp.at[theirs], pair_in.at[d], pair_send.at[d], pair_recv.at[d], (sibling, tz))
        pairs[d].start()
        if waiting is not None:
            reduce_pair(waiting)
        waiting = d
    reduce_pair(0)
    mine = pl.ds(pl.multiple_of(dp * block, block), block)
    total = t_exp[mine, :] + pair_in[0]
    for d in (1, 2, 3):
        planes[d].wait()
        total = total + plane_in[d - 1].astype(jnp.float32)
    s_exp[0:block, :] = total
    lines = []
    for k in range(1, nt):
        peer = lax.rem(tz + k, nt)
        part = pl.ds(pl.multiple_of(peer * features, features), features)
        lines.append(
            remote(s_exp.at[0:block, part], line_in.at[k - 1], line_send.at[k - 1], line_recv.at[k - 1], (dp, peer))
        )
        lines[-1].start()
    result = s_exp[0:block, pl.ds(pl.multiple_of(tz * features, features), features)]
    for k in range(1, nt):
        lines[k - 1].wait()
        result = result + line_in[k - 1]
    input_out[...] = result
    for copy in outs:
        copy.wait()
    rows_copy.wait()


def fused(n, nt, teacher_hidden, student_hidden, target_ids, teacher_head, student_head):
    block, teacher_depth = teacher_hidden.shape
    depth, width = student_head.shape
    tokens = n * block
    features = depth // nt
    rounds = (n - 1).bit_length() + (nt - 1).bit_length()
    ids = jnp.broadcast_to(target_ids.astype(jnp.float32)[None, :], (8, block))
    f32, bf16, dma = jnp.float32, jnp.bfloat16, pltpu.SemaphoreType.DMA
    anywhere = pl.BlockSpec(memory_space=pl.ANY)
    whole = pl.BlockSpec(memory_space=pltpu.VMEM)
    logit_grad, student_rows, input_grad = pl.pallas_call(
        functools.partial(kernel, n, nt, min(512, width)),
        out_shape=(
            jax.ShapeDtypeStruct((tokens, width), bf16),
            jax.ShapeDtypeStruct((tokens, depth), bf16),
            jax.ShapeDtypeStruct((block, features), f32),
        ),
        in_specs=[anywhere, anywhere, whole, anywhere, anywhere],
        out_specs=(anywhere, anywhere, whole),
        scratch_shapes=[
            pltpu.VMEM((tokens, teacher_depth), bf16),
            pltpu.VMEM((tokens, depth), bf16),
            pltpu.VMEM((n, 8, block), f32),
            pltpu.VMEM((teacher_depth, width), bf16),
            pltpu.VMEM((depth, width), bf16),
            pltpu.VMEM((tokens, width), f32),
            pltpu.VMEM((tokens, width), f32),
            pltpu.VMEM((2, 2 * n, block), f32),
            pltpu.VMEM((2 * n, block), f32),
            pltpu.VMEM((rounds, 2, 2 * n, block), f32),
            pltpu.VMEM((2 * n, block), f32),
            pltpu.VMEM((n // 2, block, depth), f32),
            pltpu.VMEM((n // 2 - 1, block, depth), bf16),
            pltpu.VMEM((nt - 1, block, features), f32),
            dma((5,)), dma((5,)),
            dma((LINKED, 2)), dma((LINKED, 2)),
            dma((n - 1,)), dma((n - 1,)),
            dma((rounds,)), dma((rounds,)),
            dma((n // 2,)), dma((n // 2,)),
            dma((n // 2 - 1,)), dma((n // 2 - 1,)),
            dma((nt - 1,)), dma((nt - 1,)),
        ],
        compiler_params=pltpu.CompilerParams(
            collective_id=0, has_side_effects=True, vmem_limit_bytes=67043328
        ),
    )(teacher_hidden, student_hidden, ids, teacher_head, student_head)
    head_grad = lax.dot_general(
        student_rows, logit_grad, (((0,), (0,)), ((), ())), preferred_element_type=jnp.float32
    )
    return head_grad, input_grad


def choose(n, nt, *arrays):
    teacher_hidden, student_hidden, _, teacher_head, student_head = arrays
    block, width = teacher_hidden.shape[0], student_head.shape[1]
    fits = (
        n == 8
        and nt in (2, 4, 8)
        and block == 128
        and width == student_head.shape[0]
        and width % 512 == 0
        and teacher_head.shape[0] >= n * block + 3 * block
    )
    return fused(n, nt, *arrays) if fits else body(*arrays)


def solution(mesh):
    placed = (
        P("dp", None),
        P("dp", None),
        P("dp"),
        P(None, ("dp", "tensor")),
        P(None, ("dp", "tensor")),
    )
    return jax.shard_map(
        functools.partial(choose, mesh.shape["dp"], mesh.shape["tensor"]),
        mesh=mesh,
        in_specs=placed,
        out_specs=(P(None, ("dp", "tensor")), P("dp", "tensor")),
        check_vma=False,
    )
```

```python
import functools

import jax
import jax.numpy as jnp
from jax import lax
from jax.experimental import pallas as pl
from jax.experimental.pallas import tpu as pltpu
from jax.sharding import PartitionSpec as P

VOCAB = 64128


def body(teacher_hidden, student_hidden, target_ids, teacher_head, student_head):
    width_cols = teacher_head.shape[1]
    first_col = (
        lax.axis_index("dp") * lax.axis_size("tensor") + lax.axis_index("tensor")
    ) * width_cols
    columns = first_col + lax.iota(jnp.int32, width_cols)
    is_real = (columns < VOCAB)[None, :]
    teacher_logits = jnp.dot(
        lax.all_gather(teacher_hidden, "dp", axis=0, tiled=True),
        teacher_head,
        preferred_element_type=jnp.float32,
    )
    teacher_logits = jnp.where(is_real, teacher_logits, jnp.float32(-1e30))
    student_rows, all_targets = (
        lax.all_gather(student_hidden, "dp", axis=0, tiled=True),
        lax.all_gather(target_ids, "dp", axis=0, tiled=True),
    )
    student_logits = jnp.where(
        is_real,
        jnp.dot(student_rows, student_head, preferred_element_type=jnp.float32),
        jnp.float32(-1e30),
    )
    peaks = jnp.stack([jnp.max(teacher_logits, axis=1), jnp.max(student_logits, axis=1)])
    totals = jnp.stack(
        [
            jnp.sum(jnp.exp(teacher_logits - peaks[0][:, None]), axis=1),
            jnp.sum(jnp.exp(student_logits - peaks[1][:, None]), axis=1),
        ]
    )
    table = lax.all_gather(jnp.concatenate([peaks, totals]), ("dp", "tensor"), axis=0)
    top = jnp.max(table[:, :2], axis=0)
    teacher_total, student_total = jnp.sum(table[:, 2:] * jnp.exp(table[:, :2] - top), axis=0)
    teacher_expo = jnp.exp(teacher_logits - top[0][:, None])
    student_expo = jnp.exp(student_logits - top[1][:, None])
    teacher_probs = teacher_expo / teacher_total[:, None]
    student_probs = student_expo / student_total[:, None]
    onehot = (all_targets[:, None] == columns[None, :]).astype(jnp.float32)
    logit_grad = (2.0 * student_probs - teacher_probs - onehot).astype(jnp.bfloat16)
    head_grad = lax.dot_general(
        student_rows, logit_grad, (((0,), (0,)), ((), ())), preferred_element_type=jnp.float32
    )
    own_rows = lax.psum_scatter(
        lax.dot_general(
            logit_grad, student_head, (((1,), (1,)), ((), ())), preferred_element_type=jnp.float32
        ),
        "dp",
        scatter_dimension=0,
        tiled=True,
    )
    input_grad = lax.psum_scatter(own_rows, "tensor", scatter_dimension=1, tiled=True)
    return (head_grad, input_grad)


MESH = pl.DeviceIdType.MESH
LINKED = 9


def as_column(row):
    return jnp.transpose(jnp.broadcast_to(row, (row.shape[1], row.shape[1])))[:, :1]


def as_row(column):
    return jnp.transpose(jnp.broadcast_to(column, (column.shape[0], column.shape[0])))[:1, :]


def kernel(
    n, nt, tile,
    teacher_in, student_in, ids_in, teacher_head, student_head,
    grad_out, rows_out, *refs,
):
    part_outs = refs[:nt]
    (
        t_rows, s_rows, ids, t_w, s_w, t_exp, s_exp,
        stats, local_peak, stats_in, scale, pair_in, plane_in,
        local_sem, out_sem, gather_send, gather_recv, ids_send, ids_recv,
        stats_send, stats_recv, pair_send, pair_recv, plane_send, plane_recv,
    ) = refs[nt:]
    block = teacher_in.shape[0]
    pair = 2 * block
    width = t_w.shape[1]
    depth = s_w.shape[0]
    features = depth // nt
    dp = lax.axis_index("dp")
    tz = lax.axis_index("tensor")
    chip, core = dp // 2, dp % 2

    def flip(value, bit):
        return value + bit - 2 * bit * ((value // bit) % 2)

    def other(d):
        out = chip
        for bit in (1, 2):
            if d & bit:
                out = flip(out, bit)
        return out

    sibling = chip * 2 + 1 - core
    near = (other(1) * 2 + core, other(2) * 2 + core)

    barrier = pltpu.get_barrier_semaphore()
    for k in range(1, n):
        pl.semaphore_signal(barrier, inc=1, device_id=(lax.rem(dp + k, n), tz), device_id_type=MESH)
    for k in range(1, nt):
        pl.semaphore_signal(barrier, inc=1, device_id=(dp, lax.rem(tz + k, nt)), device_id_type=MESH)
    pl.semaphore_wait(barrier, n - 1 + nt - 1)

    def at(index, start=0, size=None):
        return pl.ds(pl.multiple_of(index * block + start, block // 2), block if size is None else size)

    def remote(source, target, send, recv, device):
        return pltpu.make_async_remote_copy(
            src_ref=source, dst_ref=target, send_sem=send, recv_sem=recv,
            device_id=device, device_id_type=MESH,
        )

    def message(k, rows, device, from_input=False):
        pieces = []
        for a, (given, held) in enumerate(((student_in, s_rows), (teacher_in, t_rows))):
            source = given if from_input else held.at[rows]
            pieces.append(
                remote(source, held.at[rows], gather_send.at[k, a], gather_recv.at[k, a], (device, tz))
            )
        return pieces

    own = at(dp)
    msgs = [message(0, own, sibling, True), message(1, own, near[0], True), message(2, own, near[1], True)]
    for a in range(2):
        for m in (msgs[1], msgs[2], msgs[0]):
            m[a].start()
    loads = [
        pltpu.make_async_copy(student_in, s_rows.at[own], local_sem.at[0]),
        pltpu.make_async_copy(student_head, s_w, local_sem.at[1]),
        pltpu.make_async_copy(teacher_in, t_rows.at[own], local_sem.at[2]),
        pltpu.make_async_copy(teacher_head, t_w, local_sem.at[3]),
        pltpu.make_async_copy(ids_in, ids.at[dp], local_sem.at[4]),
    ]
    for load in loads:
        load.start()
    id_msgs = []
    for k in range(1, n):
        id_msgs.append(
            remote(ids_in, ids.at[dp], ids_send.at[k - 1], ids_recv.at[k - 1], (lax.rem(dp + k, n), tz))
        )
        id_msgs[-1].start()

    first_col = (dp * nt + tz) * width

    def forward(which, d):
        rows_ref, w_ref, exp_ref = ((s_rows, s_w, s_exp), (t_rows, t_w, t_exp))[which]
        target = other(d)
        rows = pl.ds(pl.multiple_of(target * pair, pair), pair)

        def multiply(j, peak):
            cols = pl.ds(pl.multiple_of(j * tile, tile), tile)
            z = jnp.dot(rows_ref[rows, :], w_ref[:, cols], preferred_element_type=jnp.float32)
            col = first_col + j * tile + lax.broadcasted_iota(jnp.int32, (1, tile), 1)
            z = jnp.where(col < VOCAB, z, jnp.float32(-1e30))
            exp_ref[rows, cols] = z
            return jnp.maximum(peak, jnp.max(z, axis=1, keepdims=True))

        peak = lax.fori_loop(0, width // tile, multiply, jnp.full((pair, 1), -jnp.inf, jnp.float32))

        def exponential(j, total):
            cols = pl.ds(pl.multiple_of(j * tile, tile), tile)
            e = jnp.exp(exp_ref[rows, cols] - peak)
            exp_ref[rows, cols] = e
            return total + jnp.sum(e, axis=1, keepdims=True)

        total = lax.fori_loop(0, width // tile, exponential, jnp.zeros((pair, 1), jnp.float32))
        for h in range(2):
            slot = pl.ds((1 - which) * n + target * 2 + h, 1)
            stats[0, slot, :] = as_row(peak[h * block : (h + 1) * block])
            stats[1, slot, :] = as_row(total[h * block : (h + 1) * block])

    half = block // 2
    across = other(3) * 2 + core
    msgs.append(message(3, at(near[0], 0, half), near[1]))
    msgs.append(message(4, at(near[1], half, half), near[0]))
    msgs.append(message(5, at(near[0]), sibling))
    msgs.append(message(6, at(near[1]), sibling))
    msgs.append(message(7, at(across, 0, half), sibling))
    msgs.append(message(8, at(across, half, half), sibling))

    def pass_on(a):
        for k in (1, 2):
            msgs[k][a].wait_recv()
            msgs[k + 2][a].start()
            msgs[k + 4][a].start()

    def pass_across(a):
        for k in (3, 4):
            msgs[k][a].wait_recv()
            msgs[k + 4][a].start()

    loads[0].wait()
    loads[1].wait()
    msgs[0][0].wait_recv()
    forward(0, 0)
    pass_on(0)
    loads[2].wait()
    loads[3].wait()
    msgs[0][1].wait_recv()
    forward(1, 0)
    for d in (1, 2):
        msgs[d + 4][0].wait_recv()
        forward(0, d)
    pass_on(1)
    pass_across(0)
    msgs[5][1].wait_recv()
    forward(1, 1)
    msgs[7][0].wait_recv()
    msgs[8][0].wait_recv()
    forward(0, 3)
    msgs[6][1].wait_recv()
    pass_across(1)
    forward(1, 2)
    msgs[7][1].wait_recv()
    msgs[8][1].wait_recv()
    forward(1, 3)
    rows_copy = pltpu.make_async_copy(s_rows, rows_out, out_sem.at[4])
    rows_copy.start()

    local_peak[...] = stats[0]
    partners = []
    bit = 1
    while bit < n:
        partners.append((flip(dp, bit), tz))
        bit *= 2
    bit = 1
    while bit < nt:
        partners.append((dp, flip(tz, bit)))
        bit *= 2
    for r, partner in enumerate(partners):
        swap = remote(stats, stats_in.at[r], stats_send.at[r], stats_recv.at[r], partner)
        swap.start()
        swap.wait()
        mine, theirs = stats[0], stats_in[r, 0]
        top = jnp.maximum(mine, theirs)
        stats[1] = stats[1] * jnp.exp(mine - top) + stats_in[r, 1] * jnp.exp(theirs - top)
        stats[0] = top
    scale[...] = jnp.exp(local_peak[...] - stats[0]) / stats[1]
    loads[4].wait()
    for m in id_msgs:
        m.wait()
    for m in msgs:
        for piece in m:
            piece.wait_send()

    tokens = t_rows.shape[0]
    grads = t_w
    outs, pairs, planes = [], {}, {}

    def plane_rows(d):
        return pl.ds(tokens + (d - 1) * block, block)

    def reduce_pair(d):
        pairs[d].wait()
        mine = pl.ds(pl.multiple_of(other(d) * pair + core * block, block), block)
        if d:
            grads[plane_rows(d), :] = (t_exp[mine, :] + pair_in[d]).astype(jnp.bfloat16)
            planes[d] = remote(
                grads.at[plane_rows(d)], plane_in.at[d - 1],
                plane_send.at[d - 1], plane_recv.at[d - 1], (other(d) * 2 + core, tz),
            )
            planes[d].start()

    waiting = None
    for d in (3, 1, 2, 0):
        target = other(d)
        rows = pl.ds(pl.multiple_of(target * pair, pair), pair)

        def column_of(ref_row):
            return jnp.concatenate([as_column(ref_row(h)) for h in range(2)], axis=0)

        t_scale = column_of(lambda h: scale[pl.ds(target * 2 + h, 1), :])
        s_scale = 2.0 * column_of(lambda h: scale[pl.ds(n + target * 2 + h, 1), :])
        wanted = column_of(lambda h: ids[target * 2 + h][:1, :])

        def gradient(j, carry):
            cols = pl.ds(pl.multiple_of(j * tile, tile), tile)
            col = (first_col + j * tile + lax.broadcasted_iota(jnp.int32, (1, tile), 1)).astype(jnp.float32)
            g = s_exp[rows, cols] * s_scale - t_exp[rows, cols] * t_scale
            g = g - jnp.where(wanted == col, 1.0, 0.0)
            grads[rows, cols] = g.astype(jnp.bfloat16)
            return carry

        lax.fori_loop(0, width // tile, gradient, 0)
        outs.append(pltpu.make_async_copy(grads.at[rows], grad_out.at[rows], out_sem.at[d]))
        outs[-1].start()

        def back(j, carry):
            cols = pl.ds(pl.multiple_of(j * tile, tile), tile)
            t_exp[rows, cols] = lax.dot_general(
                grads[rows, :], s_w[cols, :], (((1,), (1,)), ((), ())), preferred_element_type=jnp.float32
            )
            return carry

        lax.fori_loop(0, depth // tile, back, 0)
        theirs = pl.ds(pl.multiple_of(target * pair + (1 - core) * block, block), block)
        pairs[d] = remote(t_exp.at[theirs], pair_in.at[d], pair_send.at[d], pair_recv.at[d], (sibling, tz))
        pairs[d].start()
        if waiting is not None:
            reduce_pair(waiting)
        waiting = d
    reduce_pair(0)
    mine = pl.ds(pl.multiple_of(dp * block, block), block)
    total = t_exp[mine, :] + pair_in[0]
    for d in (1, 2, 3):
        planes[d].wait()
        total = total + plane_in[d - 1].astype(jnp.float32)
    s_exp[0:block, :] = total
    for k in range(nt):
        part = pl.ds(pl.multiple_of(lax.rem(tz + k, nt) * features, features), features)
        part_outs[k][...] = s_exp[0:block, part]
    for copy in outs:
        copy.wait()
    rows_copy.wait()


def fused(n, nt, teacher_hidden, student_hidden, target_ids, teacher_head, student_head):
    block, teacher_depth = teacher_hidden.shape
    depth, width = student_head.shape
    tokens = n * block
    features = depth // nt
    rounds = (n - 1).bit_length() + (nt - 1).bit_length()
    ids = jnp.broadcast_to(target_ids.astype(jnp.float32)[None, :], (8, block))
    f32, bf16, dma = jnp.float32, jnp.bfloat16, pltpu.SemaphoreType.DMA
    anywhere = pl.BlockSpec(memory_space=pl.ANY)
    whole = pl.BlockSpec(memory_space=pltpu.VMEM)
    logit_grad, student_rows, *parts = pl.pallas_call(
        functools.partial(kernel, n, nt, min(512, width)),
        out_shape=(
            jax.ShapeDtypeStruct((tokens, width), bf16),
            jax.ShapeDtypeStruct((tokens, depth), bf16),
        )
        + (jax.ShapeDtypeStruct((block, features), f32),) * nt,
        in_specs=[anywhere, anywhere, whole, anywhere, anywhere],
        out_specs=(anywhere, anywhere) + (whole,) * nt,
        scratch_shapes=[
            pltpu.VMEM((tokens, teacher_depth), bf16),
            pltpu.VMEM((tokens, depth), bf16),
            pltpu.VMEM((n, 8, block), f32),
            pltpu.VMEM((teacher_depth, width), bf16),
            pltpu.VMEM((depth, width), bf16),
            pltpu.VMEM((tokens, width), f32),
            pltpu.VMEM((tokens, width), f32),
            pltpu.VMEM((2, 2 * n, block), f32),
            pltpu.VMEM((2 * n, block), f32),
            pltpu.VMEM((rounds, 2, 2 * n, block), f32),
            pltpu.VMEM((2 * n, block), f32),
            pltpu.VMEM((n // 2, block, depth), f32),
            pltpu.VMEM((n // 2 - 1, block, depth), bf16),
            dma((5,)), dma((5,)),
            dma((LINKED, 2)), dma((LINKED, 2)),
            dma((n - 1,)), dma((n - 1,)),
            dma((rounds,)), dma((rounds,)),
            dma((n // 2,)), dma((n // 2,)),
            dma((n // 2 - 1,)), dma((n // 2 - 1,)),
        ],
        compiler_params=pltpu.CompilerParams(
            collective_id=0, has_side_effects=True, vmem_limit_bytes=67043328
        ),
    )(teacher_hidden, student_hidden, ids, teacher_head, student_head)
    head_grad = lax.dot_general(
        student_rows, logit_grad, (((0,), (0,)), ((), ())), preferred_element_type=jnp.float32
    )
    input_grad = parts[0]
    for k in range(1, nt):
        ring = [(i, (i + k) % nt) for i in range(nt)]
        input_grad = input_grad + lax.ppermute(parts[k], "tensor", ring)
    return head_grad, input_grad


def choose(n, nt, *arrays):
    teacher_hidden, student_hidden, _, teacher_head, student_head = arrays
    block, width = teacher_hidden.shape[0], student_head.shape[1]
    fits = (
        n == 8
        and nt in (2, 4, 8)
        and block == 128
        and width == student_head.shape[0]
        and width % 512 == 0
        and teacher_head.shape[0] >= n * block + 3 * block
    )
    return fused(n, nt, *arrays) if fits else body(*arrays)


def solution(mesh):
    placed = (
        P("dp", None),
        P("dp", None),
        P("dp"),
        P(None, ("dp", "tensor")),
        P(None, ("dp", "tensor")),
    )
    return jax.shard_map(
        functools.partial(choose, mesh.shape["dp"], mesh.shape["tensor"]),
        mesh=mesh,
        in_specs=placed,
        out_specs=(P(None, ("dp", "tensor")), P("dp", "tensor")),
        check_vma=False,
    )
```
